32 devices in a mesh: grp: 4 (over y, core), dev: 8 (over z, x).
Axes of the slice: x: 2, y: 2, z: 4, core: 2. Of those that a mesh axis runs over, the one named last changes fastest.
Arguments:
- objective: float32 [4, 8, 1024, 256], P('grp', 'dev'), may hold values from -24 to 24
- schur: float32 [4, 8, 1024, 1024], P('grp', 'dev')
- local_inverse: float32 [4, 8, 1024, 1024], P('grp', 'dev')
- coarse_basis: float32 [4, 8, 64, 1024], P('grp', 'dev'), may hold values from -0.09375 to 0.09375
- coarse_inverse: float32 [4, 8, 32, 1024], P(None, 'dev', None, 'grp')
- stiffness: int32 [4, 8, 1024], P('grp', 'dev'), may hold values from 1 to 8
- face_rows: int32 [4, 8, 4, 256], P('grp', 'dev'), may hold values from -1 to 1023, as said below
- coarse_map: int32 [4, 8, 64], P('grp', 'dev'), may hold values from 0 to 127
Outputs:
- adjoint: float32 [4, 8, 1024, 256], P('grp', 'dev')
The draws below stay inside these ranges and needn't reach their ends.
Inputs may be any that keep to these rules, and one draw needn't show every extreme that they name: `face_rows`: slot k of face p names the local row of the k-th row that the subdomain shares with its neighbour across face p, or -1; the live slots of a face come first, and the neighbour lists the same shared rows in the same order in its opposite face. The live slots of a subdomain name its rows 0 to n - 1 once each, n at most 1024, and at least one subdomain has all 1024 rows. Faces at the ends of the layout are empty; a face that joins two subdomains has 1 to 256 rows. `coarse_map`: entry e of subdomain (g, d) names the coarse dof (e // 32, d, e % 32), owned by the subdomain at grp index e // 32 of the same dev index.
All inputs are finite; a program needn't handle non-finite values.
Results may differ from the reference program's by a relative error of at most 0.0003.
Values sent between devices are 32-bit elements; how exact they have to be, the bound alone decides.
A program may use at most 64 MiB of HBM per device.

```python
import math
import jax
import jax.numpy as jnp
from jax import lax

INTERFACE = 1024
FACE_ROWS = 256
COLUMNS = 256
OWNED = 32
COARSE_LOCAL = 64
SWEEPS = 2
COARSE = 1024
N_GRP = 4
N_DEV = 8


def dominant(key, order, low, high, spread):
    noise_key, diagonal_key = jax.random.split(key)
    shape = (N_GRP, N_DEV, order, order)
    off_part = jax.random.normal(noise_key, shape) * (spread / math.sqrt(order))
    diagonal = jax.random.uniform(diagonal_key, (N_GRP, N_DEV, order), minval=low, maxval=high)
    identity = jnp.eye(order, dtype=bool)
    return jnp.where(identity, off_part + diagonal[:, :, None, :], off_part)


def draw_schur(key, part):
    return dominant(jax.random.fold_in(key, 11), INTERFACE, 2.0, 4.0, 0.8)


def draw_local_inverse(key, part):
    return dominant(jax.random.fold_in(key, 23), INTERFACE, 0.12, 0.25, 0.05)


def draw_coarse_inverse(key, part):
    noise_key, diagonal_key = jax.random.split(jax.random.fold_in(key, 37))
    total = OWNED * N_GRP * N_DEV
    shape = (N_GRP, N_DEV, OWNED, total)
    off_part = jax.random.normal(noise_key, shape) * (0.5 / math.sqrt(total))
    diagonal = jax.random.uniform(diagonal_key, (N_GRP, N_DEV, OWNED), minval=0.5, maxval=1.5)
    row_number = (jnp.arange(N_GRP)[:, None, None] * N_DEV + jnp.arange(N_DEV)[None, :, None]) * OWNED + jnp.arange(OWNED)[None, None, :]
    identity = row_number[..., None] == jnp.arange(total)[None, None, None, :]
    return jnp.where(identity, off_part + diagonal[..., None], off_part)


def draw_face_rows(key, part):
    across_key, downward_key, priority_key = jax.random.split(jax.random.fold_in(key, 53), 3)
    lowest = max(FACE_ROWS // 4, 1)
    across = jax.random.randint(across_key, (N_GRP, N_DEV), lowest, FACE_ROWS + 1)
    downward = jax.random.randint(downward_key, (N_GRP, N_DEV), lowest, FACE_ROWS + 1)
    across = across.at[1, 0].set(FACE_ROWS).at[1, 1].set(FACE_ROWS)
    downward = downward.at[0, 1].set(FACE_ROWS).at[1, 1].set(FACE_ROWS)
    grp_pos = jnp.arange(N_GRP)[:, None]
    dev_pos = jnp.arange(N_DEV)[None, :]
    minus_dev = jnp.where(dev_pos > 0, jnp.roll(across, 1, axis=1), 0)
    plus_dev = jnp.where(dev_pos < N_DEV - 1, across, 0)
    minus_grp = jnp.where(grp_pos > 0, jnp.roll(downward, 1, axis=0), 0)
    plus_grp = jnp.where(grp_pos < N_GRP - 1, downward, 0)
    counts = jnp.stack([minus_dev, plus_dev, minus_grp, plus_grp], axis=2)
    live_slot = jnp.arange(FACE_ROWS)[None, None, None, :] < counts[..., None]
    live_slot = live_slot.reshape(N_GRP, N_DEV, 4 * FACE_ROWS)
    split_keys = jax.random.split(priority_key, N_GRP * N_DEV)
    priority = jax.vmap(lambda single: jax.random.permutation(single, 4 * FACE_ROWS))(split_keys)
    priority = priority.reshape(N_GRP, N_DEV, 4 * FACE_ROWS).astype(jnp.int32)
    ranking_key = jnp.where(live_slot, priority, 4 * FACE_ROWS + priority)
    ordering = jnp.argsort(ranking_key, axis=-1, stable=True)
    row_rank = jnp.argsort(ordering, axis=-1, stable=True).astype(jnp.int32)
    slot_rows = jnp.where(live_slot, row_rank, -1).astype(jnp.int32)
    return slot_rows.reshape(N_GRP, N_DEV, 4, FACE_ROWS)


def touch_ends(drawn, rng, low, high):
    extent = drawn.shape
    spot = [jax.random.randint(jax.random.fold_in(rng, axis), (), 0, extent[axis]) for axis in range(len(extent))]
    drawn = drawn.at[tuple(spot)].set(low)
    longest = extent.index(max(extent))
    spot[longest] = (spot[longest] + 1) % extent[longest]
    return drawn.at[tuple(spot)].set(high)


def shard_levels(stream_key, dims, cuts, least, top_value):
    factor_of = 1.0
    for dim, parts in cuts:
        heights = jax.random.uniform(jax.random.fold_in(jax.random.fold_in(stream_key, 6), dim), (parts,), jnp.float32, least / len(cuts), top_value / len(cuts))
        factor_of = factor_of * jnp.repeat(jnp.exp(heights), dims[dim] // parts).reshape((-1,) + (1,) * (len(dims) - 1 - dim))
    return factor_of


def gaussian(own_key, dims, scale, reach, cuts=(), kind=jnp.bfloat16):
    values = scale * jax.random.normal(own_key, dims, jnp.float32)
    if cuts:
        values = values * shard_levels(own_key, dims, cuts, -0.22, 0.18)
    return jnp.clip(values, -reach, reach).astype(kind)


def setup_inputs(seed: int = 0) -> dict:
    key_of = jax.random.split(jax.random.key(seed), 9)
    return {
        "objective": gaussian(key_of[0], (N_GRP, N_DEV, INTERFACE, COLUMNS), 4.0, 24.0, ((0, 4), (1, 8)), jnp.float32),
        "schur": draw_schur(jax.random.fold_in(key_of[8], 71), 0),
        "local_inverse": draw_local_inverse(jax.random.fold_in(key_of[8], 71), 0),
        "coarse_basis": gaussian(key_of[3], (N_GRP, N_DEV, COARSE_LOCAL, INTERFACE), (4 * INTERFACE) ** -0.5, 0.09375, ((0, 4), (1, 8)), jnp.float32),
        "coarse_inverse": draw_coarse_inverse(jax.random.fold_in(key_of[8], 71), 0),
        "stiffness": touch_ends(jax.random.randint(key_of[5], (N_GRP, N_DEV, INTERFACE), 1, 9), jax.random.fold_in(key_of[5], 1), 1, 8).astype(jnp.int32),
        "face_rows": draw_face_rows(jax.random.fold_in(key_of[8], 71), 0),
        "coarse_map": touch_ends(jax.random.randint(key_of[7], (N_GRP, N_DEV, COARSE_LOCAL), 0, N_GRP * OWNED), jax.random.fold_in(key_of[7], 1), 0, (N_GRP * OWNED) - 1).astype(jnp.int32),
    }


def slot_inverse(slot_rows):
    slot_count = 4 * FACE_ROWS
    slot_index = jnp.where(slot_rows < 0, INTERFACE, slot_rows).reshape(-1).astype(jnp.int32)
    empty = jnp.full((INTERFACE,), slot_count, jnp.int32)
    return empty.at[slot_index].set(jnp.arange(slot_count, dtype=jnp.int32), mode="drop")


def pack_one(values, slot_rows):
    slot_index = jnp.where(slot_rows < 0, INTERFACE, slot_rows).reshape(-1).astype(jnp.int32)
    return jnp.take(values, slot_index, axis=0, mode="fill", fill_value=0)


def unpack_one(received, inverse):
    return jnp.take(received, inverse, axis=0, mode="fill", fill_value=0)


def neighbour(values, face_rows, inverse):
    packed = jax.vmap(jax.vmap(pack_one))(values, face_rows)
    packed = packed.reshape(N_GRP, N_DEV, 4, FACE_ROWS, values.shape[-1])
    blank = jnp.zeros_like(packed[:, :, 0])
    from_left = jnp.concatenate([blank[:, :1], packed[:, :-1, 1]], axis=1)
    from_right = jnp.concatenate([packed[:, 1:, 0], blank[:, :1]], axis=1)
    from_above = jnp.concatenate([blank[:1], packed[:-1, :, 3]], axis=0)
    from_below = jnp.concatenate([packed[1:, :, 2], blank[:1]], axis=0)
    received = jnp.stack([from_left, from_right, from_above, from_below], axis=2)
    received = received.reshape(N_GRP, N_DEV, 4 * FACE_ROWS, values.shape[-1])
    return jax.vmap(jax.vmap(unpack_one))(received, inverse)


def reference(objective, schur, local_inverse, coarse_basis, coarse_inverse, stiffness, face_rows, coarse_map):
    highest = lax.Precision.HIGHEST
    inverse = jax.vmap(jax.vmap(slot_inverse))(face_rows)
    live_rows = (inverse < 4 * FACE_ROWS).astype(jnp.float32)[..., None]
    multiplicity = stiffness.astype(jnp.float32)[..., None]
    weight = live_rows * multiplicity / (multiplicity + neighbour(multiplicity, face_rows, inverse))
    onehot = (coarse_map[..., None] == jnp.arange(N_GRP * OWNED, dtype=jnp.int32)).astype(jnp.float32)
    inverse_matrix = coarse_inverse.reshape(COARSE, COARSE)
    adjoint = jnp.zeros(objective.shape, jnp.float32)
    for sweep_index in range(SWEEPS):
        if sweep_index == 0:
            remain = objective
        else:
            remain = objective - jnp.einsum("gdrc,gdrk->gdck", schur, adjoint, precision=highest)
        residual = live_rows * (remain + neighbour(remain, face_rows, inverse))
        weighted = weight * residual
        local_terms = jnp.einsum("gdlr,gdrk->gdlk", coarse_basis, weighted, precision=highest)
        spread_terms = jnp.einsum("gdlo,gdlk->gdok", onehot, local_terms, precision=highest)
        column_sums = jnp.sum(spread_terms, axis=0)
        coarse_residual = column_sums.reshape(N_DEV, N_GRP, OWNED, -1).transpose(1, 0, 2, 3).reshape(COARSE, -1)
        coarse_solution = jnp.dot(inverse_matrix.T, coarse_residual, precision=highest, preferred_element_type=jnp.float32)
        column_solution = coarse_solution.reshape(N_GRP, N_DEV, OWNED, -1).transpose(1, 0, 2, 3).reshape(N_DEV, N_GRP * OWNED, -1)
        local_solution = jnp.einsum("gdlo,dok->gdlk", onehot, column_solution, precision=highest)
        correction = jnp.einsum("gdlr,gdlk->gdrk", coarse_basis, local_solution, precision=highest)
        local_part = jnp.einsum("gdrc,gdrk->gdck", local_inverse, weighted, precision=highest)
        update = weight * (local_part + correction)
        adjoint = adjoint + update + neighbour(update, face_rows, inverse)
    return adjoint
```

```python
import functools

import jax
import jax.numpy as jnp
from jax import lax
from jax.experimental import pallas as pl
from jax.experimental.pallas import tpu as pltpu
from jax.sharding import PartitionSpec as P

SWEEPS = 2
LANES = 128
KC = LANES // 2
ORDER = (
    "B0 C1 P2 b0", "M0 X0 E0 C2", "W0 W1 R0 P3", "C3 L0 W2 R1", "l0 k0 O0 R2",
    "W3 O1 U0 R3", "L1 U1 O2 l1", "k1 S0 U2 O3", "A0 U3 a0 z0", "A1 C1+ a1 z1",
    "W0+ C2+ W1+ R0+", "P3+ C3+ L0+ W2+", "R1+ l0+ k0+ O0+", "R2+ W3+ O1+ U0+", "R3+ L1+ U1+ O2+",
    "l1+ k1+ U2+ O3+", "U3+ A0+ A1+",
)
MESH = pl.DeviceIdType.MESH
F32, BF16 = jnp.float32, jnp.bfloat16


def split(value):
    high = value.astype(BF16)
    return high, (value - high.astype(F32)).astype(BF16)


def dot(left, right, left_dim, right_dim):
    return lax.dot_general(
        left, right, (((left_dim,), (right_dim,)), ((), ())), preferred_element_type=F32
    )


def stacked(value):
    return jnp.concatenate(split(value), axis=0)


def fold(value):
    half = value.shape[0] // 2
    return value[:half] + value[half:]


def fold_lanes(value):
    half = value.shape[1] // 2
    return value[:, :half] + value[:, half:]


def left_lanes(shape):
    return lax.broadcasted_iota(jnp.int32, shape, len(shape) - 1) < KC


def fold_pack(top, bottom):
    top = top + pltpu.roll(top, KC, 1)
    bottom = bottom + pltpu.roll(bottom, KC, 1)
    return jnp.where(left_lanes(top.shape), top, bottom)


def kernel(
    G, D, NC,
    obj_hbm, schur_hbm, local_hbm, basis_hbm, tile_hbm, mult, faces, cmap, out,
    pt, mhat, mrecv, wgt, xs, rc, zh, hats, wide, bhat, ehat, oneh, mmat, gath, part, scat, sol,
    obj, basis, tile, raw, schur, local,
    load_sem, m_send, m_recv, o_send, o_recv, f_send, f_recv,
    g_send, g_recv, p_send, p_recv, s_send, s_recv,
):
    g, d = lax.axis_index("grp"), lax.axis_index("dev")
    R, F = pt.shape[1], pt.shape[2]
    dofs, wide_cols = tile.shape
    terms = basis.shape[0]
    own = dofs // G
    half_terms, half_own = terms // 2, own // 2
    pair_cols = 2 * KC
    face_ids = range(4)
    arrivals = (2, 3, 0, 1)
    has = [d > 0, d < D - 1, g > 0, g < G - 1]
    near = [
        (g, lax.max(d - 1, 0)),
        (g, lax.min(d + 1, D - 1)),
        (lax.max(g - 1, 0), d),
        (lax.min(g + 1, G - 1), d),
    ]

    def load(index):
        source, dest = loads[index]
        return pltpu.make_async_copy(source, dest, load_sem.at[index])

    obj_pairs = [pl.ds(q * pair_cols, pair_cols) for q in range(NC // 2)]
    loads = [(obj_hbm.at[:, at], obj.at[:, at]) for at in obj_pairs]
    BASIS, TILE, LOCAL, SCHUR = range(NC // 2, NC // 2 + 4)
    loads += [(basis_hbm, basis), (tile_hbm, tile), (local_hbm, raw.at[0]), (schur_hbm, raw.at[1])]

    def remote(src, dst, send, recv, device):
        return pltpu.make_async_remote_copy(
            src_ref=src, dst_ref=dst, send_sem=send, recv_sem=recv,
            device_id=device, device_id_type=MESH,
        )

    barrier = pltpu.get_barrier_semaphore()
    grp_peers = [lax.rem(g + j, G) for j in range(1, G)]
    dev_peers = [lax.rem(d + j, D) for j in range(1, D)]
    for peer in grp_peers:
        pl.semaphore_signal(barrier, inc=1, device_id=(peer, d), device_id_type=MESH)
    for peer in dev_peers:
        pl.semaphore_signal(barrier, inc=1, device_id=(g, peer), device_id_type=MESH)

    for index in range(len(loads)):
        load(index).start()

    def m_copy(p, landing):
        return remote(mhat.at[p], mrecv.at[landing], m_send.at[p], m_recv.at[landing], near[p])

    def face_copy(e, c, p, landing):
        return remote(
            xs.at[e, c, p], rc.at[e, c, landing], f_send.at[e, c, p], f_recv.at[e, c, landing],
            near[p],
        )

    def grp_copy(buf, send, recv, j, slot):
        peer = lax.rem(g + j, G)
        return remote(buf.at[slot], buf.at[slot], send.at[j], recv.at[j], (peer, d))

    def dev_copy(t, c, j, slot):
        peer = lax.rem(d + j, D)
        return remote(
            part.at[t, c, peer], scat.at[t, c, slot], p_send.at[t, c, j], p_recv.at[t, c, j],
            (g, peer),
        )

    odd = lax.rem(d, 2) == 1
    near_side = (odd, jnp.logical_not(odd))

    def send_plane(e, c):
        for p in face_ids:
            here = jnp.logical_and(has[p], near_side[p]) if p < 2 else has[p]
            pl.when(here)(lambda p=p: face_copy(e, c, p, p ^ 1).start())

    def send_cross(e, c):
        for p in (0, 1):
            here = jnp.logical_and(has[p], jnp.logical_not(near_side[p]))
            pl.when(here)(lambda p=p: face_copy(e, c, p, p ^ 1).start())

    def send(e, c):
        if (e, c, "P") not in held:
            send_plane(e, c)
        if (e, c, "C") not in held:
            send_cross(e, c)

    def wait_face(e, c, p):
        pl.when(has[p])(lambda: face_copy(e, c, p, p).wait_recv())

    plan = [(item[0], int(item[1]), len(item) - 2) for item in " ".join(ORDER).split()]
    held = {(2 * t + kind.islower(), c, kind.upper()) for kind, c, t in plan if kind in "PCpc"}
    rows = lax.broadcasted_iota(jnp.int32, (R, F), 0)
    mrow = jnp.broadcast_to(mult[...].astype(F32), (8, R)).astype(BF16)
    member = lax.broadcasted_iota(jnp.int32, (dofs, terms), 0)
    oneh[g] = (member == cmap[...]).astype(F32).T

    def gather(q, faces_now):
        turned = stacked(obj[:, q * pair_cols : (q + 1) * pair_cols].T)
        for p in faces_now:
            value = fold(dot(turned, pt[p], 1, 0))
            for i in range(2):
                xs[0, 2 * q + i, p] = value[i * KC : (i + 1) * KC]

    def place(faces_now):
        for p in faces_now:
            pt[p] = (rows == faces[p : p + 1, :]).astype(F32).astype(BF16)
            mhat[p] = dot(mrow, pt[p], 1, 0)

    place(face_ids)
    load(0).wait()
    gather(0, face_ids)
    pl.semaphore_wait(barrier, G + D - 2)
    for p in face_ids:
        pl.when(has[p])(lambda p=p: m_copy(p, p ^ 1).start())
    send(0, 0)
    for j in range(1, G):
        grp_copy(oneh, o_send, o_recv, j, g).start()
    send(0, 1)
    for q in range(1, NC // 2):
        load(q).wait()
        gather(q, face_ids)
        send(0, 2 * q)
        send(0, 2 * q + 1)

    def setup_b(t, i):
        for p in face_ids:

            @pl.when(jnp.logical_not(has[p]))
            def _():
                mrecv[p] = jnp.zeros(mrecv.shape[1:], F32)
                for e in range(2 * SWEEPS):
                    for c in range(NC):
                        rc[e, c, p] = jnp.zeros(rc.shape[3:], F32)

        load(BASIS).wait()
        base = stacked(basis[...])
        for p in face_ids:
            bhat[p] = dot(base, pt[p], 1, 0).astype(BF16)

    def setup_w(t, i):
        for p in face_ids:
            pl.when(has[p])(lambda p=p: m_copy(p, p).wait_recv())
            mine = mhat[p]
            wgt[p] = jnp.where(mine > 0, mine / jnp.where(mine > 0, mine + mrecv[p], 1.0), 0.0)

    def setup_e(t, i):
        block = G * half_own
        dof = (lax.rem(member, block) // half_own) * own + (member // block) * half_own
        dof += lax.rem(member, half_own)
        spread = (dof == cmap[...]).astype(F32).astype(BF16)
        double = jnp.concatenate([spread, spread], axis=1)
        for p in face_ids:
            ehat[0, p], ehat[1, p] = split(dot(double, bhat[p], 1, 0))

    def setup_m(t, i):
        for j in range(1, G):
            grp_copy(oneh, o_send, o_recv, j, lax.rem(g + G - j, G)).wait_recv()
        picks = jnp.concatenate(
            [
                oneh[:, :half_terms].reshape(G * half_terms, dofs),
                oneh[:, half_terms:].reshape(G * half_terms, dofs),
            ],
            axis=0,
        ).astype(BF16)
        load(TILE).wait()
        tile_high, tile_low = split(tile[...])
        mmat[:wide_cols] = dot(picks, tile_high, 1, 0).T.astype(BF16)
        mmat[wide_cols:] = dot(picks, tile_low, 1, 0).T.astype(BF16)

    def split_matrix(index, dest):
        block = 128

        def body(i, carry):
            at = pl.ds(pl.multiple_of(i * block, block), block)
            high, low = split(raw[index, at, :])
            dest[0, at, :] = high
            dest[1, at, :] = low
            return carry

        lax.fori_loop(0, R // block, body, 0)

    def setup_x(t, i):
        load(LOCAL).wait()
        split_matrix(0, local)

    def setup_s(t, i):
        load(SCHUR).wait()
        split_matrix(1, schur)

    def scatter(pieces):
        total = None
        for p in arrivals:
            term = dot(pieces(p), pt[p], 1, 1)
            total = term if total is None else total + term
        wide[0] = total.astype(BF16)

    def blocks(matrix, part_index):
        block = F
        half = R // block // 2

        def body(i, carry):
            at = pl.ds(pl.multiple_of(i * block, block), block)
            product = fold(dot(wide[0], matrix[0, :, at], 1, 0))
            product += dot(wide[0, :pair_cols], matrix[1, :, at], 1, 0)
            wide[1, :, at] = stacked(product)
            return carry

        lax.fori_loop(part_index * half, (part_index + 1) * half, body, 0)

    def to_slots(p):
        return fold(dot(wide[1], pt[p], 1, 0))

    def stage_w(t, c):
        first = 2 * t
        q, at = c // 2, (c % 2) * KC
        total = None
        for p in arrivals:
            wait_face(first, c, p)
            high, low = split(wgt[p][0:1, :] * (xs[first, c, p] + rc[first, c, p]))
            hats[q, p, at : at + KC] = high
            hats[q, p, pair_cols + at : pair_cols + at + KC] = low
            term = dot(bhat[p], jnp.concatenate([high, low], axis=0), 1, 1)
            total = term if total is None else total + term
        total = fold(total)
        gath[t, c, g] = fold_pack(total[:half_terms], total[half_terms:])
        for j in range(1, G):
            grp_copy(gath.at[t, c], g_send.at[t, c], g_recv.at[t, c], j, g).start()

    def stage_l(t, q):
        scatter(lambda p: hats[q, p])
        blocks(local, 0)

    def stage_l2(t, q):
        blocks(local, 1)

    def stage_l3(t, q):
        for p in face_ids:
            zh[q, p] = to_slots(p)

    def stage_r(t, c):
        for j in range(1, G):
            grp_copy(
                gath.at[t, c], g_send.at[t, c], g_recv.at[t, c], j, lax.rem(g + G - j, G)
            ).wait_recv()
        value = gath[t, c].reshape(G * half_terms, LANES)
        high = value.astype(BF16).astype(F32)
        low = value - high
        left = left_lanes(value.shape)
        every = jnp.concatenate(
            [
                jnp.where(left, high, pltpu.roll(low, KC, 1)),
                jnp.where(left, pltpu.roll(high, KC, 1), low),
            ],
            axis=0,
        ).astype(BF16)
        product = fold(dot(mmat[...], every, 1, 0)).reshape(D, own, LANES)
        top = product[:, :half_own].reshape(D * half_own, LANES)
        bottom = product[:, half_own:].reshape(D * half_own, LANES)
        part[t, c] = fold_pack(top, bottom).reshape(part.shape[2:])
        for j in range(1, D):
            dev_copy(t, c, j, d).start()

    def stage_o(t, c):
        owned = part[t, c, d]
        for j in range(1, D):
            source = lax.rem(d + D - j, D)
            dev_copy(t, c, j, source).wait_recv()
            owned += scat[t, c, source]
        sol[t, c, g] = owned
        for j in range(1, G):
            grp_copy(sol.at[t, c], s_send.at[t, c], s_recv.at[t, c], j, g).start()

    def stage_u(t, c):
        second = 2 * t + 1
        q, at = c // 2, (c % 2) * KC
        for j in range(1, G):
            grp_copy(
                sol.at[t, c], s_send.at[t, c], s_recv.at[t, c], j, lax.rem(g + G - j, G)
            ).wait_recv()
        value = sol[t, c].reshape(G * half_own, LANES)
        value = jnp.concatenate([value, pltpu.roll(value, KC, 1)], axis=0)
        solved = stacked(value.T[:KC])
        for p in face_ids:
            fix = fold(dot(solved, ehat[0, p], 1, 0)) + dot(solved[:KC], ehat[1, p], 1, 0)
            xs[second, c, p] = wgt[p][0:1, :] * (zh[q, p, at : at + KC] + fix)
        send(second, c)

    def stage_a(t, q):
        second = 2 * t + 1
        chunks = (2 * q, 2 * q + 1)

        def assembled(p):
            values = []
            for c in chunks:
                wait_face(second, c, p)
                values.append(xs[second, c, p] + rc[second, c, p])
            value = jnp.concatenate(values, axis=0)
            if t > 0:
                value += zh[NC // 2 + q, p]
            if t < SWEEPS - 1:
                zh[NC // 2 + q, p] = value
            return stacked(value)

        if t < SWEEPS - 1:
            scatter(assembled)
            blocks(schur, 0)
        else:
            total = None
            for p in arrivals:
                term = dot(pt[p], assembled(p), 1, 1)
                total = term if total is None else total + term
            out[:, q * pair_cols : (q + 1) * pair_cols] = fold_lanes(total)

    def stage_a2(t, q):
        blocks(schur, 1)

    def stage_a3(t, q):
        third = 2 * t + 2
        for p in face_ids:
            moved = to_slots(p)
            for i in range(2):
                xs[third, 2 * q + i, p] = xs[0, 2 * q + i, p] - moved[i * KC : (i + 1) * KC]
        for c in (2 * q, 2 * q + 1):
            send(third, c)

    stages = dict(
        B=setup_b, b=setup_w, E=setup_e, M=setup_m, X=setup_x, S=setup_s,
        W=stage_w, L=stage_l, l=stage_l2, k=stage_l3, R=stage_r, O=stage_o, U=stage_u,
        A=stage_a, a=stage_a2, z=stage_a3,
        P=lambda t, c: send_plane(2 * t, c), C=lambda t, c: send_cross(2 * t, c),
        p=lambda t, c: send_plane(2 * t + 1, c), c=lambda t, c: send_cross(2 * t + 1, c),
    )
    for kind, c, t in plan:
        stages[kind](t, c)

    for p in face_ids:

        @pl.when(has[p])
        def _():
            m_copy(p, p).wait_send()
            for e in range(2 * SWEEPS):
                for c in range(NC):
                    face_copy(e, c, p, p).wait_send()

    for j in range(1, G):
        grp_copy(oneh, o_send, o_recv, j, g).wait_send()
    for t in range(SWEEPS):
        for c in range(NC):
            for j in range(1, G):
                grp_copy(gath.at[t, c], g_send.at[t, c], g_recv.at[t, c], j, g).wait_send()
                grp_copy(sol.at[t, c], s_send.at[t, c], s_recv.at[t, c], j, g).wait_send()
            for j in range(1, D):
                dev_copy(t, c, j, d).wait_send()


def on_device(
    G, D, objective, schur, local_inverse, coarse_basis, coarse_inverse, stiffness, face_rows,
    coarse_map,
):
    R, K = objective.shape[2:]
    F = face_rows.shape[3]
    terms = coarse_basis.shape[2]
    tile = coarse_inverse.reshape(-1, coarse_inverse.shape[3])
    dofs = tile.shape[0]
    own = coarse_inverse.shape[2]
    NC = K // KC
    E = 2 * SWEEPS
    vmem = pl.BlockSpec(memory_space=pltpu.VMEM)
    hbm = pl.BlockSpec(memory_space=pl.ANY)
    dma = pltpu.SemaphoreType.DMA
    result = pl.pallas_call(
        functools.partial(kernel, G, D, NC),
        out_shape=jax.ShapeDtypeStruct((R, K), F32),
        in_specs=[hbm, hbm, hbm, hbm, hbm, vmem, vmem, vmem],
        out_specs=vmem,
        scratch_shapes=[
            pltpu.VMEM((4, R, F), BF16),
            pltpu.VMEM((4, 8, F), F32),
            pltpu.VMEM((4, 8, F), F32),
            pltpu.VMEM((4, 8, F), F32),
            pltpu.VMEM((E, NC, 4, KC, F), F32),
            pltpu.VMEM((E, NC, 4, KC, F), F32),
            pltpu.VMEM((NC, 4, 2 * KC, F), F32),
            pltpu.VMEM((NC // 2, 4, 4 * KC, F), BF16),
            pltpu.VMEM((2, 4 * KC, R), BF16),
            pltpu.VMEM((4, 2 * terms, F), BF16),
            pltpu.VMEM((2, 4, dofs, F), BF16),
            pltpu.VMEM((G, terms, dofs), F32),
            pltpu.VMEM((2 * tile.shape[1], G * terms), BF16),
            pltpu.VMEM((SWEEPS, NC, G, terms // 2, LANES), F32),
            pltpu.VMEM((SWEEPS, NC, D, own // 2, LANES), F32),
            pltpu.VMEM((SWEEPS, NC, D, own // 2, LANES), F32),
            pltpu.VMEM((SWEEPS, NC, G, own // 2, LANES), F32),
            pltpu.VMEM((R, K), F32),
            pltpu.VMEM((terms, R), F32),
            pltpu.VMEM(tile.shape, F32),
            pltpu.VMEM((2, R, R), F32),
            pltpu.VMEM((2, R, R), BF16),
            pltpu.VMEM((2, R, R), BF16),
            dma((NC // 2 + 4,)),
            dma((4,)),
            dma((4,)),
            dma((G,)),
            dma((G,)),
            dma((E, NC, 4)),
            dma((E, NC, 4)),
            dma((SWEEPS, NC, G)),
            dma((SWEEPS, NC, G)),
            dma((SWEEPS, NC, D)),
            dma((SWEEPS, NC, D)),
            dma((SWEEPS, NC, G)),
            dma((SWEEPS, NC, G)),
        ],
        compiler_params=pltpu.CompilerParams(
            collective_id=0, has_side_effects=True, vmem_limit_bytes=60 * 1024 * 1024
        ),
        name="sweeps",
    )(
        objective[0, 0], schur[0, 0], local_inverse[0, 0], coarse_basis[0, 0], tile,
        stiffness[0], face_rows[0, 0], coarse_map[0],
    )
    return result[None, None]


def solution(mesh):
    return jax.shard_map(
        functools.partial(on_device, mesh.shape["grp"], mesh.shape["dev"]),
        mesh=mesh,
        in_specs=(
            P("grp", "dev", None, None),
            P("grp", "dev", None, None),
            P("grp", "dev", None, None),
            P("grp", "dev", None, None),
            P(None, "dev", None, "grp"),
            P("grp", "dev", None),
            P("grp", "dev", None, None),
            P("grp", "dev", None),
        ),
        out_specs=P("grp", "dev", None, None),
        check_vma=False,
    )
```

```python
import functools

import jax
import jax.numpy as jnp
from jax import lax
from jax.experimental import pallas as pl
from jax.experimental.pallas import tpu as pltpu
from jax.sharding import PartitionSpec as P

SWEEPS = 2
LANES = 128
KC = LANES // 2
ORDER = (
    "B0 C1 P2 b0", "M0 X0 E0 C2", "W0 W1 P3 C3", "R0 L0 W2 R1", "l0 S0 k0 O0",
    "R2 W3 O1 U0", "R3 O2 U1 L1", "l1 k1 O3 U2", "U3 A0 a0 z0", "A1 C1+ a1 z1",
    "W0+ C2+ W1+ R0+", "P3+ C3+ L0+ R1+", "W2+ l0+ k0+ O0+", "R2+ W3+ O1+ U0+", "R3+ O2+ U1+ L1+",
    "l1+ k1+ O3+ U2+", "A0+ U3+ A1+",
)
MESH = pl.DeviceIdType.MESH
F32, BF16 = jnp.float32, jnp.bfloat16


def split(value):
    high = value.astype(BF16)
    return high, (value - high.astype(F32)).astype(BF16)


def dot(left, right, left_dim, right_dim):
    return lax.dot_general(
        left, right, (((left_dim,), (right_dim,)), ((), ())), preferred_element_type=F32
    )


def stacked(value):
    return jnp.concatenate(split(value), axis=0)


def fold(value):
    half = value.shape[0] // 2
    return value[:half] + value[half:]


def fold_lanes(value):
    half = value.shape[1] // 2
    return value[:, :half] + value[:, half:]


def left_lanes(shape):
    return lax.broadcasted_iota(jnp.int32, shape, len(shape) - 1) < KC


def fold_pack(top, bottom):
    top = top + pltpu.roll(top, KC, 1)
    bottom = bottom + pltpu.roll(bottom, KC, 1)
    return jnp.where(left_lanes(top.shape), top, bottom)


def kernel(
    G, D, NC,
    obj_hbm, schur_hbm, local_hbm, basis_hbm, tile_hbm, mult, faces, cmap, out,
    pt, mhat, mrecv, wgt, xs, rc, zh, hats, wide, bhat, ehat, oneh, mmat, gath, part, scat, sol,
    obj, basis, tile, raw, schur, local,
    load_sem, m_send, m_recv, o_send, o_recv, f_send, f_recv,
    g_send, g_recv, p_send, p_recv, s_send, s_recv,
):
    g, d = lax.axis_index("grp"), lax.axis_index("dev")
    R, F = pt.shape[1], pt.shape[2]
    dofs, wide_cols = tile.shape
    terms = basis.shape[0]
    own = dofs // G
    half_terms, half_own = terms // 2, own // 2
    pair_cols = 2 * KC
    face_ids = range(4)
    arrivals = (2, 3, 0, 1)
    has = [d > 0, d < D - 1, g > 0, g < G - 1]
    near = [
        (g, lax.max(d - 1, 0)),
        (g, lax.min(d + 1, D - 1)),
        (lax.max(g - 1, 0), d),
        (lax.min(g + 1, G - 1), d),
    ]

    def load(index):
        source, dest = loads[index]
        return pltpu.make_async_copy(source, dest, load_sem.at[index])

    obj_pairs = [pl.ds(q * pair_cols, pair_cols) for q in range(NC // 2)]
    loads = [(obj_hbm.at[:, at], obj.at[:, at]) for at in obj_pairs]
    BASIS, TILE, LOCAL, SCHUR = range(NC // 2, NC // 2 + 4)
    loads += [(basis_hbm, basis), (tile_hbm, tile), (local_hbm, raw.at[0]), (schur_hbm, raw.at[1])]

    def remote(src, dst, send, recv, device):
        return pltpu.make_async_remote_copy(
            src_ref=src, dst_ref=dst, send_sem=send, recv_sem=recv,
            device_id=device, device_id_type=MESH,
        )

    barrier = pltpu.get_barrier_semaphore()
    grp_peers = [lax.rem(g + j, G) for j in range(1, G)]
    dev_peers = [lax.rem(d + j, D) for j in range(1, D)]
    for peer in grp_peers:
        pl.semaphore_signal(barrier, inc=1, device_id=(peer, d), device_id_type=MESH)
    for peer in dev_peers:
        pl.semaphore_signal(barrier, inc=1, device_id=(g, peer), device_id_type=MESH)

    for index in range(len(loads)):
        load(index).start()

    def m_copy(p, landing):
        return remote(mhat.at[p], mrecv.at[landing], m_send.at[p], m_recv.at[landing], near[p])

    def face_copy(e, c, p, landing):
        return remote(
            xs.at[e, c, p], rc.at[e, c, landing], f_send.at[e, c, p], f_recv.at[e, c, landing],
            near[p],
        )

    def grp_copy(buf, send, recv, j, slot):
        peer = lax.rem(g + j, G)
        return remote(buf.at[slot], buf.at[slot], send.at[j], recv.at[j], (peer, d))

    def dev_copy(t, c, j, slot):
        peer = lax.rem(d + j, D)
        return remote(
            part.at[t, c, peer], scat.at[t, c, slot], p_send.at[t, c, j], p_recv.at[t, c, j],
            (g, peer),
        )

    odd = lax.rem(d, 2) == 1
    near_side = (odd, jnp.logical_not(odd))

    def send_plane(e, c):
        for p in face_ids:
            here = jnp.logical_and(has[p], near_side[p]) if p < 2 else has[p]
            pl.when(here)(lambda p=p: face_copy(e, c, p, p ^ 1).start())

    def send_cross(e, c):
        for p in (0, 1):
            here = jnp.logical_and(has[p], jnp.logical_not(near_side[p]))
            pl.when(here)(lambda p=p: face_copy(e, c, p, p ^ 1).start())

    def send(e, c):
        if (e, c, "P") not in held:
            send_plane(e, c)
        if (e, c, "C") not in held:
            send_cross(e, c)

    def wait_face(e, c, p):
        pl.when(has[p])(lambda: face_copy(e, c, p, p).wait_recv())

    plan = [(item[0], int(item[1]), len(item) - 2) for item in " ".join(ORDER).split()]
    held = {(2 * t + kind.islower(), c, kind.upper()) for kind, c, t in plan if kind in "PCpc"}
    rows = lax.broadcasted_iota(jnp.int32, (R, F), 0)
    mrow = jnp.broadcast_to(mult[...].astype(F32), (8, R)).astype(BF16)
    member = lax.broadcasted_iota(jnp.int32, (dofs, terms), 0)
    oneh[g] = (member == cmap[...]).astype(F32).T

    def gather(q, faces_now):
        turned = stacked(obj[:, q * pair_cols : (q + 1) * pair_cols].T)
        for p in faces_now:
            value = fold(dot(turned, pt[p], 1, 0))
            for i in range(2):
                xs[0, 2 * q + i, p] = value[i * KC : (i + 1) * KC]

    def place(faces_now):
        for p in faces_now:
            pt[p] = (rows == faces[p : p + 1, :]).astype(F32).astype(BF16)
            mhat[p] = dot(mrow, pt[p], 1, 0)

    place(face_ids)
    load(0).wait()
    gather(0, face_ids)
    pl.semaphore_wait(barrier, G + D - 2)
    for p in face_ids:
        pl.when(has[p])(lambda p=p: m_copy(p, p ^ 1).start())
    send(0, 0)
    for j in range(1, G):
        grp_copy(oneh, o_send, o_recv, j, g).start()
    send(0, 1)
    for q in range(1, NC // 2):
        load(q).wait()
        gather(q, face_ids)
        send(0, 2 * q)
        send(0, 2 * q + 1)

    def setup_b(t, i):
        for p in face_ids:

            @pl.when(jnp.logical_not(has[p]))
            def _():
                mrecv[p] = jnp.zeros(mrecv.shape[1:], F32)
                for e in range(2 * SWEEPS):
                    for c in range(NC):
                        rc[e, c, p] = jnp.zeros(rc.shape[3:], F32)

        load(BASIS).wait()
        base = stacked(basis[...])
        for p in face_ids:
            bhat[p] = dot(base, pt[p], 1, 0).astype(BF16)

    def setup_w(t, i):
        for p in face_ids:
            pl.when(has[p])(lambda p=p: m_copy(p, p).wait_recv())
            mine = mhat[p]
            wgt[p] = jnp.where(mine > 0, mine / jnp.where(mine > 0, mine + mrecv[p], 1.0), 0.0)

    def setup_e(t, i):
        block = G * half_own
        dof = (lax.rem(member, block) // half_own) * own + (member // block) * half_own
        dof += lax.rem(member, half_own)
        spread = (dof == cmap[...]).astype(F32).astype(BF16)
        double = jnp.concatenate([spread, spread], axis=1)
        for p in face_ids:
            ehat[0, p], ehat[1, p] = split(dot(double, bhat[p], 1, 0))

    def setup_m(t, i):
        for j in range(1, G):
            grp_copy(oneh, o_send, o_recv, j, lax.rem(g + G - j, G)).wait_recv()
        picks = jnp.concatenate(
            [
                oneh[:, :half_terms].reshape(G * half_terms, dofs),
                oneh[:, half_terms:].reshape(G * half_terms, dofs),
            ],
            axis=0,
        ).astype(BF16)
        load(TILE).wait()
        tile_high, tile_low = split(tile[...])
        mmat[:wide_cols] = dot(picks, tile_high, 1, 0).T.astype(BF16)
        mmat[wide_cols:] = dot(picks, tile_low, 1, 0).T.astype(BF16)

    def split_matrix(index, dest):
        block = 128

        def body(i, carry):
            at = pl.ds(pl.multiple_of(i * block, block), block)
            high, low = split(raw[index, at, :])
            dest[0, at, :] = high
            dest[1, at, :] = low
            return carry

        lax.fori_loop(0, R // block, body, 0)

    def setup_x(t, i):
        load(LOCAL).wait()
        split_matrix(0, local)

    def setup_s(t, i):
        load(SCHUR).wait()
        split_matrix(1, schur)

    def scatter(pieces):
        total = None
        for p in arrivals:
            term = dot(pieces(p), pt[p], 1, 1)
            total = term if total is None else total + term
        wide[0] = total.astype(BF16)

    def blocks(matrix, part_index):
        block = F
        half = R // block // 2

        def body(i, carry):
            at = pl.ds(pl.multiple_of(i * block, block), block)
            product = fold(dot(wide[0], matrix[0, :, at], 1, 0))
            product += dot(wide[0, :pair_cols], matrix[1, :, at], 1, 0)
            wide[1, :, at] = stacked(product)
            return carry

        lax.fori_loop(part_index * half, (part_index + 1) * half, body, 0)

    def to_slots(p):
        return fold(dot(wide[1], pt[p], 1, 0))

    def stage_w(t, c):
        first = 2 * t
        q, at = c // 2, (c % 2) * KC
        total = None
        for p in arrivals:
            wait_face(first, c, p)
            high, low = split(wgt[p][0:1, :] * (xs[first, c, p] + rc[first, c, p]))
            hats[q, p, at : at + KC] = high
            hats[q, p, pair_cols + at : pair_cols + at + KC] = low
            term = dot(bhat[p], jnp.concatenate([high, low], axis=0), 1, 1)
            total = term if total is None else total + term
        total = fold(total)
        gath[t, c, g] = fold_pack(total[:half_terms], total[half_terms:])
        for j in range(1, G):
            grp_copy(gath.at[t, c], g_send.at[t, c], g_recv.at[t, c], j, g).start()

    def stage_l(t, q):
        scatter(lambda p: hats[q, p])
        blocks(local, 0)

    def stage_l2(t, q):
        blocks(local, 1)

    def stage_l3(t, q):
        for p in face_ids:
            zh[q, p] = to_slots(p)

    def stage_r(t, c):
        for j in range(1, G):
            grp_copy(
                gath.at[t, c], g_send.at[t, c], g_recv.at[t, c], j, lax.rem(g + G - j, G)
            ).wait_recv()
        value = gath[t, c].reshape(G * half_terms, LANES)
        high = value.astype(BF16).astype(F32)
        low = value - high
        left = left_lanes(value.shape)
        every = jnp.concatenate(
            [
                jnp.where(left, high, pltpu.roll(low, KC, 1)),
                jnp.where(left, pltpu.roll(high, KC, 1), low),
            ],
            axis=0,
        ).astype(BF16)
        product = fold(dot(mmat[...], every, 1, 0)).reshape(D, own, LANES)
        top = product[:, :half_own].reshape(D * half_own, LANES)
        bottom = product[:, half_own:].reshape(D * half_own, LANES)
        part[t, c] = fold_pack(top, bottom).reshape(part.shape[2:])
        for j in range(1, D):
            dev_copy(t, c, j, d).start()

    def stage_o(t, c):
        owned = part[t, c, d]
        for j in range(1, D):
            source = lax.rem(d + D - j, D)
            dev_copy(t, c, j, source).wait_recv()
            owned += scat[t, c, source]
        sol[t, c, g] = owned
        for j in range(1, G):
            grp_copy(sol.at[t, c], s_send.at[t, c], s_recv.at[t, c], j, g).start()

    def stage_u(t, c):
        second = 2 * t + 1
        q, at = c // 2, (c % 2) * KC
        for j in range(1, G):
            grp_copy(
                sol.at[t, c], s_send.at[t, c], s_recv.at[t, c], j, lax.rem(g + G - j, G)
            ).wait_recv()
        value = sol[t, c].reshape(G * half_own, LANES)
        value = jnp.concatenate([value, pltpu.roll(value, KC, 1)], axis=0)
        solved = stacked(value.T[:KC])
        for p in face_ids:
            fix = fold(dot(solved, ehat[0, p], 1, 0)) + dot(solved[:KC], ehat[1, p], 1, 0)
            xs[second, c, p] = wgt[p][0:1, :] * (zh[q, p, at : at + KC] + fix)
        send(second, c)

    def stage_a(t, q):
        second = 2 * t + 1
        chunks = (2 * q, 2 * q + 1)

        def assembled(p):
            values = []
            for c in chunks:
                wait_face(second, c, p)
                values.append(xs[second, c, p] + rc[second, c, p])
            value = jnp.concatenate(values, axis=0)
            if t > 0:
                value += zh[NC // 2 + q, p]
            if t < SWEEPS - 1:
                zh[NC // 2 + q, p] = value
            return stacked(value)

        if t < SWEEPS - 1:
            scatter(assembled)
            blocks(schur, 0)
        else:
            total = None
            for p in arrivals:
                term = dot(pt[p], assembled(p), 1, 1)
                total = term if total is None else total + term
            out[:, q * pair_cols : (q + 1) * pair_cols] = fold_lanes(total)

    def stage_a2(t, q):
        blocks(schur, 1)

    def stage_a3(t, q):
        third = 2 * t + 2
        for p in face_ids:
            moved = to_slots(p)
            for i in range(2):
                xs[third, 2 * q + i, p] = xs[0, 2 * q + i, p] - moved[i * KC : (i + 1) * KC]
        for c in (2 * q, 2 * q + 1):
            send(third, c)

    stages = dict(
        B=setup_b, b=setup_w, E=setup_e, M=setup_m, X=setup_x, S=setup_s,
        W=stage_w, L=stage_l, l=stage_l2, k=stage_l3, R=stage_r, O=stage_o, U=stage_u,
        A=stage_a, a=stage_a2, z=stage_a3,
        P=lambda t, c: send_plane(2 * t, c), C=lambda t, c: send_cross(2 * t, c),
        p=lambda t, c: send_plane(2 * t + 1, c), c=lambda t, c: send_cross(2 * t + 1, c),
    )
    for kind, c, t in plan:
        stages[kind](t, c)

    for p in face_ids:

        @pl.when(has[p])
        def _():
            m_copy(p, p).wait_send()
            for e in range(2 * SWEEPS):
                for c in range(NC):
                    face_copy(e, c, p, p).wait_send()

    for j in range(1, G):
        grp_copy(oneh, o_send, o_recv, j, g).wait_send()
    for t in range(SWEEPS):
        for c in range(NC):
            for j in range(1, G):
                grp_copy(gath.at[t, c], g_send.at[t, c], g_recv.at[t, c], j, g).wait_send()
                grp_copy(sol.at[t, c], s_send.at[t, c], s_recv.at[t, c], j, g).wait_send()
            for j in range(1, D):
                dev_copy(t, c, j, d).wait_send()


def on_device(
    G, D, objective, schur, local_inverse, coarse_basis, coarse_inverse, stiffness, face_rows,
    coarse_map,
):
    R, K = objective.shape[2:]
    F = face_rows.shape[3]
    terms = coarse_basis.shape[2]
    tile = coarse_inverse.reshape(-1, coarse_inverse.shape[3])
    dofs = tile.shape[0]
    own = coarse_inverse.shape[2]
    NC = K // KC
    E = 2 * SWEEPS
    vmem = pl.BlockSpec(memory_space=pltpu.VMEM)
    hbm = pl.BlockSpec(memory_space=pl.ANY)
    dma = pltpu.SemaphoreType.DMA
    result = pl.pallas_call(
        functools.partial(kernel, G, D, NC),
        out_shape=jax.ShapeDtypeStruct((R, K), F32),
        in_specs=[hbm, hbm, hbm, hbm, hbm, vmem, vmem, vmem],
        out_specs=vmem,
        scratch_shapes=[
            pltpu.VMEM((4, R, F), BF16),
            pltpu.VMEM((4, 8, F), F32),
            pltpu.VMEM((4, 8, F), F32),
            pltpu.VMEM((4, 8, F), F32),
            pltpu.VMEM((E, NC, 4, KC, F), F32),
            pltpu.VMEM((E, NC, 4, KC, F), F32),
            pltpu.VMEM((NC, 4, 2 * KC, F), F32),
            pltpu.VMEM((NC // 2, 4, 4 * KC, F), BF16),
            pltpu.VMEM((2, 4 * KC, R), BF16),
            pltpu.VMEM((4, 2 * terms, F), BF16),
            pltpu.VMEM((2, 4, dofs, F), BF16),
            pltpu.VMEM((G, terms, dofs), F32),
            pltpu.VMEM((2 * tile.shape[1], G * terms), BF16),
            pltpu.VMEM((SWEEPS, NC, G, terms // 2, LANES), F32),
            pltpu.VMEM((SWEEPS, NC, D, own // 2, LANES), F32),
            pltpu.VMEM((SWEEPS, NC, D, own // 2, LANES), F32),
            pltpu.VMEM((SWEEPS, NC, G, own // 2, LANES), F32),
            pltpu.VMEM((R, K), F32),
            pltpu.VMEM((terms, R), F32),
            pltpu.VMEM(tile.shape, F32),
            pltpu.VMEM((2, R, R), F32),
            pltpu.VMEM((2, R, R), BF16),
            pltpu.VMEM((2, R, R), BF16),
            dma((NC // 2 + 4,)),
            dma((4,)),
            dma((4,)),
            dma((G,)),
            dma((G,)),
            dma((E, NC, 4)),
            dma((E, NC, 4)),
            dma((SWEEPS, NC, G)),
            dma((SWEEPS, NC, G)),
            dma((SWEEPS, NC, D)),
            dma((SWEEPS, NC, D)),
            dma((SWEEPS, NC, G)),
            dma((SWEEPS, NC, G)),
        ],
        compiler_params=pltpu.CompilerParams(
            collective_id=0, has_side_effects=True, vmem_limit_bytes=60 * 1024 * 1024
        ),
        name="sweeps",
    )(
        objective[0, 0], schur[0, 0], local_inverse[0, 0], coarse_basis[0, 0], tile,
        stiffness[0], face_rows[0, 0], coarse_map[0],
    )
    return result[None, None]


def solution(mesh):
    return jax.shard_map(
        functools.partial(on_device, mesh.shape["grp"], mesh.shape["dev"]),
        mesh=mesh,
        in_specs=(
            P("grp", "dev", None, None),
            P("grp", "dev", None, None),
            P("grp", "dev", None, None),
            P("grp", "dev", None, None),
            P(None, "dev", None, "grp"),
            P("grp", "dev", None),
            P("grp", "dev", None, None),
            P("grp", "dev", None),
        ),
        out_specs=P("grp", "dev", None, None),
        check_vma=False,
    )
```

```python
import functools

import jax
import jax.numpy as jnp
from jax import lax
from jax.experimental import pallas as pl
from jax.experimental.pallas import tpu as pltpu
from jax.sharding import PartitionSpec as P

SWEEPS = 2
LANES = 128
KC = LANES // 2
ORDER = (
    "B0 C1 P2 b0", "M0 X0 E0 C2", "W0 W1 P3 C3", "R0 L0 W2 R1", "l0 S0 k0 O0",
    "R2 W3 O1 U0", "R3 O2 U1 L1", "l1 k1 O3 U2", "U3 A0 a0 z0", "A1 C1+ a1 z1",
    "W0+ C2+ W1+ R0+", "P3+ C3+ L0+ R1+", "W2+ l0+ k0+ O0+", "R2+ W3+ O1+ U0+", "R3+ O2+ U1+ L1+",
    "l1+ k1+ O3+ U2+", "A0+ U3+ A1+",
)
MESH = pl.DeviceIdType.MESH
F32, BF16 = jnp.float32, jnp.bfloat16


def split(value):
    high = value.astype(BF16)
    return high, (value - high.astype(F32)).astype(BF16)


def dot(left, right, left_dim, right_dim):
    return lax.dot_general(
        left, right, (((left_dim,), (right_dim,)), ((), ())), preferred_element_type=F32
    )


def stacked(value):
    return jnp.concatenate(split(value), axis=0)


def fold(value):
    half = value.shape[0] // 2
    return value[:half] + value[half:]


def fold_lanes(value):
    half = value.shape[1] // 2
    return value[:, :half] + value[:, half:]


def left_lanes(shape):
    return lax.broadcasted_iota(jnp.int32, shape, len(shape) - 1) < KC


def fold_pack(top, bottom):
    top = top + pltpu.roll(top, KC, 1)
    bottom = bottom + pltpu.roll(bottom, KC, 1)
    return jnp.where(left_lanes(top.shape), top, bottom)


def far_first(count):
    return sorted(range(1, count), key=lambda j: -min(j, count - j))


def kernel(
    G, D, NC,
    obj_hbm, schur_hbm, local_hbm, basis_hbm, tile_hbm, mult, faces, cmap, out,
    pt, mhat, mrecv, wgt, xs, rc, zh, hats, wide, bhat, ehat, oneh, mmat, gath, part, scat, sol,
    obj, basis, tile, raw, schur, local,
    load_sem, m_send, m_recv, o_send, o_recv, f_send, f_recv,
    g_send, g_recv, p_send, p_recv, s_send, s_recv,
):
    g, d = lax.axis_index("grp"), lax.axis_index("dev")
    R, F = pt.shape[1], pt.shape[2]
    dofs, wide_cols = tile.shape
    terms = basis.shape[0]
    own = dofs // G
    half_terms, half_own = terms // 2, own // 2
    pair_cols = 2 * KC
    face_ids = range(4)
    arrivals = (2, 3, 0, 1)
    has = [d > 0, d < D - 1, g > 0, g < G - 1]
    near = [
        (g, lax.max(d - 1, 0)),
        (g, lax.min(d + 1, D - 1)),
        (lax.max(g - 1, 0), d),
        (lax.min(g + 1, G - 1), d),
    ]

    def load(index):
        source, dest = loads[index]
        return pltpu.make_async_copy(source, dest, load_sem.at[index])

    obj_pairs = [pl.ds(q * pair_cols, pair_cols) for q in range(NC // 2)]
    loads = [(obj_hbm.at[:, at], obj.at[:, at]) for at in obj_pairs]
    BASIS, TILE, LOCAL, SCHUR = range(NC // 2, NC // 2 + 4)
    loads += [(basis_hbm, basis), (tile_hbm, tile), (local_hbm, raw.at[0]), (schur_hbm, raw.at[1])]

    def remote(src, dst, send, recv, device):
        return pltpu.make_async_remote_copy(
            src_ref=src, dst_ref=dst, send_sem=send, recv_sem=recv,
            device_id=device, device_id_type=MESH,
        )

    barrier = pltpu.get_barrier_semaphore()
    grp_peers = [lax.rem(g + j, G) for j in range(1, G)]
    dev_peers = [lax.rem(d + j, D) for j in range(1, D)]
    for peer in grp_peers:
        pl.semaphore_signal(barrier, inc=1, device_id=(peer, d), device_id_type=MESH)
    for peer in dev_peers:
        pl.semaphore_signal(barrier, inc=1, device_id=(g, peer), device_id_type=MESH)

    for index in range(len(loads)):
        load(index).start()

    def m_copy(p, landing):
        return remote(mhat.at[p], mrecv.at[landing], m_send.at[p], m_recv.at[landing], near[p])

    def face_copy(e, c, p, landing):
        return remote(
            xs.at[e, c, p], rc.at[e, c, landing], f_send.at[e, c, p], f_recv.at[e, c, landing],
            near[p],
        )

    def grp_copy(buf, send, recv, j, slot):
        peer = lax.rem(g + j, G)
        return remote(buf.at[slot], buf.at[slot], send.at[j], recv.at[j], (peer, d))

    def dev_copy(t, c, j, slot):
        peer = lax.rem(d + j, D)
        return remote(
            part.at[t, c, peer], scat.at[t, c, slot], p_send.at[t, c, j], p_recv.at[t, c, j],
            (g, peer),
        )

    odd = lax.rem(d, 2) == 1
    near_side = (odd, jnp.logical_not(odd))

    def send_plane(e, c):
        for p in face_ids:
            here = jnp.logical_and(has[p], near_side[p]) if p < 2 else has[p]
            pl.when(here)(lambda p=p: face_copy(e, c, p, p ^ 1).start())

    def send_cross(e, c):
        for p in (0, 1):
            here = jnp.logical_and(has[p], jnp.logical_not(near_side[p]))
            pl.when(here)(lambda p=p: face_copy(e, c, p, p ^ 1).start())

    def send(e, c):
        if (e, c, "P") not in held:
            send_plane(e, c)
        if (e, c, "C") not in held:
            send_cross(e, c)

    def wait_face(e, c, p):
        pl.when(has[p])(lambda: face_copy(e, c, p, p).wait_recv())

    plan = [(item[0], int(item[1]), len(item) - 2) for item in " ".join(ORDER).split()]
    held = {(2 * t + kind.islower(), c, kind.upper()) for kind, c, t in plan if kind in "PCpc"}
    rows = lax.broadcasted_iota(jnp.int32, (R, F), 0)
    mrow = jnp.broadcast_to(mult[...].astype(F32), (8, R)).astype(BF16)
    member = lax.broadcasted_iota(jnp.int32, (dofs, terms), 0)
    oneh[g] = (member == cmap[...]).astype(F32).T

    def gather(q, faces_now):
        turned = stacked(obj[:, q * pair_cols : (q + 1) * pair_cols].T)
        for p in faces_now:
            value = fold(dot(turned, pt[p], 1, 0))
            for i in range(2):
                xs[0, 2 * q + i, p] = value[i * KC : (i + 1) * KC]

    def place(faces_now):
        for p in faces_now:
            pt[p] = (rows == faces[p : p + 1, :]).astype(F32).astype(BF16)
            mhat[p] = dot(mrow, pt[p], 1, 0)

    place(face_ids)
    load(0).wait()
    gather(0, face_ids)
    pl.semaphore_wait(barrier, G + D - 2)
    for p in face_ids:
        pl.when(has[p])(lambda p=p: m_copy(p, p ^ 1).start())
    send(0, 0)
    for j in range(1, G):
        grp_copy(oneh, o_send, o_recv, j, g).start()
    send(0, 1)
    for q in range(1, NC // 2):
        load(q).wait()
        gather(q, face_ids)
        send(0, 2 * q)
        send(0, 2 * q + 1)

    def setup_b(t, i):
        for p in face_ids:

            @pl.when(jnp.logical_not(has[p]))
            def _():
                mrecv[p] = jnp.zeros(mrecv.shape[1:], F32)
                for e in range(2 * SWEEPS):
                    for c in range(NC):
                        rc[e, c, p] = jnp.zeros(rc.shape[3:], F32)

        load(BASIS).wait()
        base = stacked(basis[...])
        for p in face_ids:
            bhat[p] = dot(base, pt[p], 1, 0).astype(BF16)

    def setup_w(t, i):
        for p in face_ids:
            pl.when(has[p])(lambda p=p: m_copy(p, p).wait_recv())
            mine = mhat[p]
            wgt[p] = jnp.where(mine > 0, mine / jnp.where(mine > 0, mine + mrecv[p], 1.0), 0.0)

    def setup_e(t, i):
        block = G * half_own
        dof = (lax.rem(member, block) // half_own) * own + (member // block) * half_own
        dof += lax.rem(member, half_own)
        spread = (dof == cmap[...]).astype(F32).astype(BF16)
        double = jnp.concatenate([spread, spread], axis=1)
        for p in face_ids:
            ehat[0, p], ehat[1, p] = split(dot(double, bhat[p], 1, 0))

    def setup_m(t, i):
        for j in range(1, G):
            grp_copy(oneh, o_send, o_recv, j, lax.rem(g + G - j, G)).wait_recv()
        picks = jnp.concatenate(
            [
                oneh[:, :half_terms].reshape(G * half_terms, dofs),
                oneh[:, half_terms:].reshape(G * half_terms, dofs),
            ],
            axis=0,
        ).astype(BF16)
        load(TILE).wait()
        tile_high, tile_low = split(tile[...])
        mmat[:wide_cols] = dot(picks, tile_high, 1, 0).T.astype(BF16)
        mmat[wide_cols:] = dot(picks, tile_low, 1, 0).T.astype(BF16)

    def split_matrix(index, dest):
        block = 128

        def body(i, carry):
            at = pl.ds(pl.multiple_of(i * block, block), block)
            high, low = split(raw[index, at, :])
            dest[0, at, :] = high
            dest[1, at, :] = low
            return carry

        lax.fori_loop(0, R // block, body, 0)

    def setup_x(t, i):
        load(LOCAL).wait()
        split_matrix(0, local)

    def setup_s(t, i):
        load(SCHUR).wait()
        split_matrix(1, schur)

    def scatter(pieces):
        total = None
        for p in arrivals:
            term = dot(pieces(p), pt[p], 1, 1)
            total = term if total is None else total + term
        wide[0] = total.astype(BF16)

    def blocks(matrix, part_index):
        block = F
        half = R // block // 2

        def body(i, carry):
            at = pl.ds(pl.multiple_of(i * block, block), block)
            product = fold(dot(wide[0], matrix[0, :, at], 1, 0))
            product += dot(wide[0, :pair_cols], matrix[1, :, at], 1, 0)
            wide[1, :, at] = stacked(product)
            return carry

        lax.fori_loop(part_index * half, (part_index + 1) * half, body, 0)

    def to_slots(p):
        return fold(dot(wide[1], pt[p], 1, 0))

    def stage_w(t, c):
        first = 2 * t
        q, at = c // 2, (c % 2) * KC
        total = None
        for p in arrivals:
            wait_face(first, c, p)
            high, low = split(wgt[p][0:1, :] * (xs[first, c, p] + rc[first, c, p]))
            hats[q, p, at : at + KC] = high
            hats[q, p, pair_cols + at : pair_cols + at + KC] = low
            term = dot(bhat[p], jnp.concatenate([high, low], axis=0), 1, 1)
            total = term if total is None else total + term
        total = fold(total)
        gath[t, c, g] = fold_pack(total[:half_terms], total[half_terms:])
        for j in far_first(G):
            grp_copy(gath.at[t, c], g_send.at[t, c], g_recv.at[t, c], j, g).start()

    def stage_l(t, q):
        scatter(lambda p: hats[q, p])
        blocks(local, 0)

    def stage_l2(t, q):
        blocks(local, 1)

    def stage_l3(t, q):
        for p in face_ids:
            zh[q, p] = to_slots(p)

    def stage_r(t, c):
        for j in range(1, G):
            grp_copy(
                gath.at[t, c], g_send.at[t, c], g_recv.at[t, c], j, lax.rem(g + G - j, G)
            ).wait_recv()
        value = gath[t, c].reshape(G * half_terms, LANES)
        high = value.astype(BF16).astype(F32)
        low = value - high
        left = left_lanes(value.shape)
        every = jnp.concatenate(
            [
                jnp.where(left, high, pltpu.roll(low, KC, 1)),
                jnp.where(left, pltpu.roll(high, KC, 1), low),
            ],
            axis=0,
        ).astype(BF16)
        product = fold(dot(mmat[...], every, 1, 0)).reshape(D, own, LANES)
        top = product[:, :half_own].reshape(D * half_own, LANES)
        bottom = product[:, half_own:].reshape(D * half_own, LANES)
        part[t, c] = fold_pack(top, bottom).reshape(part.shape[2:])
        for j in far_first(D):
            dev_copy(t, c, j, d).start()

    def stage_o(t, c):
        owned = part[t, c, d]
        for j in range(1, D):
            source = lax.rem(d + D - j, D)
            dev_copy(t, c, j, source).wait_recv()
            owned += scat[t, c, source]
        sol[t, c, g] = owned
        for j in far_first(G):
            grp_copy(sol.at[t, c], s_send.at[t, c], s_recv.at[t, c], j, g).start()

    def stage_u(t, c):
        second = 2 * t + 1
        q, at = c // 2, (c % 2) * KC
        for j in range(1, G):
            grp_copy(
                sol.at[t, c], s_send.at[t, c], s_recv.at[t, c], j, lax.rem(g + G - j, G)
            ).wait_recv()
        value = sol[t, c].reshape(G * half_own, LANES)
        value = jnp.concatenate([value, pltpu.roll(value, KC, 1)], axis=0)
        solved = stacked(value.T[:KC])
        for p in face_ids:
            fix = fold(dot(solved, ehat[0, p], 1, 0)) + dot(solved[:KC], ehat[1, p], 1, 0)
            xs[second, c, p] = wgt[p][0:1, :] * (zh[q, p, at : at + KC] + fix)
        send(second, c)

    def stage_a(t, q):
        second = 2 * t + 1
        chunks = (2 * q, 2 * q + 1)

        def assembled(p):
            values = []
            for c in chunks:
                wait_face(second, c, p)
                values.append(xs[second, c, p] + rc[second, c, p])
            value = jnp.concatenate(values, axis=0)
            if t > 0:
                value += zh[NC // 2 + q, p]
            if t < SWEEPS - 1:
                zh[NC // 2 + q, p] = value
            return stacked(value)

        if t < SWEEPS - 1:
            scatter(assembled)
            blocks(schur, 0)
        else:
            total = None
            for p in arrivals:
                term = dot(pt[p], assembled(p), 1, 1)
                total = term if total is None else total + term
            out[:, q * pair_cols : (q + 1) * pair_cols] = fold_lanes(total)

    def stage_a2(t, q):
        blocks(schur, 1)

    def stage_a3(t, q):
        third = 2 * t + 2
        for p in face_ids:
            moved = to_slots(p)
            for i in range(2):
                xs[third, 2 * q + i, p] = xs[0, 2 * q + i, p] - moved[i * KC : (i + 1) * KC]
        for c in (2 * q, 2 * q + 1):
            send(third, c)

    stages = dict(
        B=setup_b, b=setup_w, E=setup_e, M=setup_m, X=setup_x, S=setup_s,
        W=stage_w, L=stage_l, l=stage_l2, k=stage_l3, R=stage_r, O=stage_o, U=stage_u,
        A=stage_a, a=stage_a2, z=stage_a3,
        P=lambda t, c: send_plane(2 * t, c), C=lambda t, c: send_cross(2 * t, c),
        p=lambda t, c: send_plane(2 * t + 1, c), c=lambda t, c: send_cross(2 * t + 1, c),
    )
    for kind, c, t in plan:
        stages[kind](t, c)

    for p in face_ids:

        @pl.when(has[p])
        def _():
            m_copy(p, p).wait_send()
            for e in range(2 * SWEEPS):
                for c in range(NC):
                    face_copy(e, c, p, p).wait_send()

    for j in range(1, G):
        grp_copy(oneh, o_send, o_recv, j, g).wait_send()
    for t in range(SWEEPS):
        for c in range(NC):
            for j in range(1, G):
                grp_copy(gath.at[t, c], g_send.at[t, c], g_recv.at[t, c], j, g).wait_send()
                grp_copy(sol.at[t, c], s_send.at[t, c], s_recv.at[t, c], j, g).wait_send()
            for j in range(1, D):
                dev_copy(t, c, j, d).wait_send()


def on_device(
    G, D, objective, schur, local_inverse, coarse_basis, coarse_inverse, stiffness, face_rows,
    coarse_map,
):
    R, K = objective.shape[2:]
    F = face_rows.shape[3]
    terms = coarse_basis.shape[2]
    tile = coarse_inverse.reshape(-1, coarse_inverse.shape[3])
    dofs = tile.shape[0]
    own = coarse_inverse.shape[2]
    NC = K // KC
    E = 2 * SWEEPS
    vmem = pl.BlockSpec(memory_space=pltpu.VMEM)
    hbm = pl.BlockSpec(memory_space=pl.ANY)
    dma = pltpu.SemaphoreType.DMA
    result = pl.pallas_call(
        functools.partial(kernel, G, D, NC),
        out_shape=jax.ShapeDtypeStruct((R, K), F32),
        in_specs=[hbm, hbm, hbm, hbm, hbm, vmem, vmem, vmem],
        out_specs=vmem,
        scratch_shapes=[
            pltpu.VMEM((4, R, F), BF16),
            pltpu.VMEM((4, 8, F), F32),
            pltpu.VMEM((4, 8, F), F32),
            pltpu.VMEM((4, 8, F), F32),
            pltpu.VMEM((E, NC, 4, KC, F), F32),
            pltpu.VMEM((E, NC, 4, KC, F), F32),
            pltpu.VMEM((NC, 4, 2 * KC, F), F32),
            pltpu.VMEM((NC // 2, 4, 4 * KC, F), BF16),
            pltpu.VMEM((2, 4 * KC, R), BF16),
            pltpu.VMEM((4, 2 * terms, F), BF16),
            pltpu.VMEM((2, 4, dofs, F), BF16),
            pltpu.VMEM((G, terms, dofs), F32),
            pltpu.VMEM((2 * tile.shape[1], G * terms), BF16),
            pltpu.VMEM((SWEEPS, NC, G, terms // 2, LANES), F32),
            pltpu.VMEM((SWEEPS, NC, D, own // 2, LANES), F32),
            pltpu.VMEM((SWEEPS, NC, D, own // 2, LANES), F32),
            pltpu.VMEM((SWEEPS, NC, G, own // 2, LANES), F32),
            pltpu.VMEM((R, K), F32),
            pltpu.VMEM((terms, R), F32),
            pltpu.VMEM(tile.shape, F32),
            pltpu.VMEM((2, R, R), F32),
            pltpu.VMEM((2, R, R), BF16),
            pltpu.VMEM((2, R, R), BF16),
            dma((NC // 2 + 4,)),
            dma((4,)),
            dma((4,)),
            dma((G,)),
            dma((G,)),
            dma((E, NC, 4)),
            dma((E, NC, 4)),
            dma((SWEEPS, NC, G)),
            dma((SWEEPS, NC, G)),
            dma((SWEEPS, NC, D)),
            dma((SWEEPS, NC, D)),
            dma((SWEEPS, NC, G)),
            dma((SWEEPS, NC, G)),
        ],
        compiler_params=pltpu.CompilerParams(
            collective_id=0, has_side_effects=True, vmem_limit_bytes=60 * 1024 * 1024
        ),
        name="sweeps",
    )(
        objective[0, 0], schur[0, 0], local_inverse[0, 0], coarse_basis[0, 0], tile,
        stiffness[0], face_rows[0, 0], coarse_map[0],
    )
    return result[None, None]


def solution(mesh):
    return jax.shard_map(
        functools.partial(on_device, mesh.shape["grp"], mesh.shape["dev"]),
        mesh=mesh,
        in_specs=(
            P("grp", "dev", None, None),
            P("grp", "dev", None, None),
            P("grp", "dev", None, None),
            P("grp", "dev", None, None),
            P(None, "dev", None, "grp"),
            P("grp", "dev", None),
            P("grp", "dev", None, None),
            P("grp", "dev", None),
        ),
        out_specs=P("grp", "dev", None, None),
        check_vma=False,
    )
```
